32 devices in a mesh: row: 8 (over y, x, core), col: 4 (over z).
Axes of the slice: x: 2, y: 2, z: 4, core: 2. Of those that a mesh axis runs over, the one named last changes fastest.
Arguments:
- amplitudes: bfloat16 [4096, 4096], P('row', 'col'), may hold values from -0.1875 to 0.1875
- factors: bfloat16 [4096, 2048], P('col', 'row'), may hold values from -0.125 to 0.125
- tile_map: int32 [16, 16], P('row', 'col'), may hold values 0 or 1
- panel_owner: int32 [2], replicated, may hold values from 0 to 3, as said below
Outputs:
- cycle_term: float32 [4096, 4096], P('row', 'col')
The draws below stay inside these ranges and needn't reach their ends.
Inputs may be any that keep to these rules, and one draw needn't show every extreme that they name: `panel_owner`: the 2 entries are distinct panel indices, and one of them is the last panel.
All inputs are finite; a program needn't handle non-finite values. No bound on the sum of `tile_map` on one device may be relied on, other than what follows from the above.
Results may differ from the reference program's by a relative error of at most 0.0029.
Values may be sent and summed in bfloat16 or wider, within the bound.
A program may use at most 64 MiB of HBM per device.

```python
import jax
import jax.numpy as jnp
from jax import lax

NAUX = 2048
STEPS = 2
PAIRS = 4096
PANEL = 1024
TILES = 16
N_COL = 4


def draw_panel_owner(key, part):
    first_key, flip_key = jax.random.split(key)
    other = jax.random.randint(first_key, (), 0, N_COL - 1)
    last = jnp.int32(N_COL - 1)
    flip = jax.random.randint(flip_key, (), 0, 2)
    forward = jnp.stack([other, last]).astype(jnp.int32)
    backward = jnp.stack([last, other]).astype(jnp.int32)
    return jnp.where(flip == 1, backward, forward)


def set_ends(array, stream_key, least, largest):
    longest = array.shape.index(max(array.shape))
    spots = []
    for shift in (0, 1):
        where = [jax.random.randint(jax.random.fold_in(stream_key, axis), (), 0, length) for axis, length in enumerate(array.shape)]
        where[longest] = (where[longest] + shift) % array.shape[longest]
        spots.append(tuple(where))
    return array.at[spots[0]].set(least).at[spots[1]].set(largest)


def level_of(stream_key, dims, cuts, smallest, largest):
    loudness, own = 1.0, jax.random.fold_in(stream_key, 6)
    for position, shards_of in cuts:
        heights = jnp.exp(jax.random.uniform(jax.random.fold_in(own, position), (shards_of,), jnp.float32, smallest / len(cuts), largest / len(cuts)))
        loudness = loudness * jnp.repeat(heights, dims[position] // shards_of).reshape([-1 if axis == position else 1 for axis in range(len(dims))])
    return loudness


def centred(own_key, shape, spread, most, shards=(), kind=jnp.bfloat16):
    factor_of = level_of(own_key, shape, shards, -0.22, 0.18) if shards else 1.0
    values = jax.random.normal(own_key, shape, jnp.float32) * spread * factor_of
    return jnp.minimum(jnp.maximum(values, -most), most).astype(kind)


def setup_inputs(seed: int = 0) -> dict:
    key_list = jax.random.split(jax.random.key(seed), 5)
    return {
        "amplitudes": centred(key_list[0], (PAIRS, PAIRS), PANEL ** -0.5, 0.1875, ((0, 8), (1, 4))),
        "factors": centred(key_list[1], (PAIRS, NAUX), NAUX ** -0.5, 0.125, ((0, 4), (1, 8))),
        "tile_map": set_ends((jax.random.randint(key_list[2], (TILES, TILES), 0, 2) < 1).astype(jnp.int32), jax.random.fold_in(key_list[2], 1), 0, 1),
        "panel_owner": draw_panel_owner(jax.random.fold_in(key_list[4], 71), 0),
    }


def keep_tiles(block, tiles):
    rows, cols = tiles.shape
    shaped = block.reshape(rows, block.shape[0] // rows, cols, block.shape[1] // cols)
    keep = tiles.astype(block.dtype)[:, None, :, None]
    return (shaped * keep).reshape(block.shape)


def reference(amplitudes, factors, tile_map, panel_owner):
    kept = keep_tiles(amplitudes, tile_map)
    width = factors.shape[0] // N_COL
    total = jnp.zeros(amplitudes.shape, jnp.float32)
    for step in range(STEPS):
        start = panel_owner[step].astype(jnp.int32) * width
        owner_factors = lax.dynamic_slice_in_dim(factors, start, width, 0)
        integrals = lax.dot_general(owner_factors, factors, (((1,), (1,)), ((), ())), preferred_element_type=jnp.float32).astype(jnp.bfloat16)
        panel = lax.dynamic_slice_in_dim(kept, start, width, 1)
        total = total + jnp.dot(panel, integrals, preferred_element_type=jnp.float32)
    return keep_tiles(total, tile_map)
```

```python
import jax
import jax.numpy as jnp
from jax import lax
from jax.sharding import PartitionSpec as P


def keep_tiles(block, tiles):
    rows, cols = tiles.shape
    shaped = block.reshape(rows, block.shape[0] // rows, cols, block.shape[1] // cols)
    keep = tiles.astype(block.dtype)[:, None, :, None]
    return (shaped * keep).reshape(block.shape)


def shards(amplitudes, factors, tile_map, panel_owner):
    mine = jnp.any(panel_owner == lax.axis_index("col"))
    kept = keep_tiles(amplitudes, tile_map * mine.astype(tile_map.dtype))
    column_factors = lax.all_gather(factors, "row", axis=1, tiled=True)
    half = jnp.dot(kept, column_factors, preferred_element_type=jnp.float32)
    half = lax.psum(half.astype(jnp.bfloat16), "col")
    total = lax.dot_general(
        half, column_factors, (((1,), (1,)), ((), ())), preferred_element_type=jnp.float32
    )
    return keep_tiles(total, tile_map)


def solution(mesh):
    in_specs = (P("row", "col"), P("col", "row"), P("row", "col"), P())
    out_specs = P("row", "col")
    return jax.shard_map(shards, mesh=mesh, in_specs=in_specs, out_specs=out_specs, check_vma=False)
```

```python
import functools

import jax
import jax.numpy as jnp
from jax import lax
from jax.experimental import pallas as pl
from jax.experimental.pallas import tpu as pltpu
from jax.sharding import PartitionSpec as P

MESH = pl.DeviceIdType.MESH
SPLITS = 2
SKEW = 2


def flip(index, bits):
    bit = 1
    while bit <= bits:
        if bits & bit:
            index = index + bit - 2 * bit * ((index // bit) % 2)
        bit *= 2
    return index


def keep_tiles(block, tiles):
    rows, cols = tiles.shape
    shaped = block.reshape(rows, block.shape[0] // rows, cols, block.shape[1] // cols)
    keep = tiles.astype(block.dtype)[:, None, :, None]
    return (shaped * keep).reshape(block.shape)


def kernel(
    cols, chips, owner_ref, tiles_ref, amp_ref, own_ref, out_ref,
    held, kept, local, down_out, down_in, up_out, up_in,
    held_send, held_recv, down_send, down_recv, up_send, up_recv,
):
    row, col = lax.axis_index("row"), lax.axis_index("col")
    core, chip = row % 2, row // 2
    partner = row + 1 - 2 * core
    blocks = 2 * chips
    steps = blocks * SPLITS
    height = kept.shape[0] // SPLITS
    first, last = col == 0, col == cols - 1

    barrier = pltpu.get_barrier_semaphore()

    def greet(**where):
        pl.semaphore_signal(barrier, inc=1, device_id=where, device_id_type=MESH)

    greet(row=partner)
    for d in range(1, chips):
        greet(row=2 * flip(chip, d) + core)

    @pl.when(col > 0)
    def _():
        greet(col=col - 1)

    @pl.when(col < cols - 1)
    def _():
        greet(col=col + 1)

    ends = jnp.where(first, 1, 0) + jnp.where(last, 1, 0)
    pl.semaphore_wait(barrier, chips + 2 - ends)

    def to_partner(src, slot):
        return pltpu.make_async_remote_copy(
            src_ref=src, dst_ref=held.at[slot], send_sem=held_send.at[slot],
            recv_sem=held_recv.at[slot], device_id={"row": partner}, device_id_type=MESH,
        )

    def to_chip(d):
        return pltpu.make_async_remote_copy(
            src_ref=own_ref, dst_ref=held.at[2 * d], send_sem=held_send.at[2 * d],
            recv_sem=held_recv.at[2 * d], device_id={"row": 2 * flip(chip, d) + core},
            device_id_type=MESH,
        )

    def down(step):
        return pltpu.make_async_remote_copy(
            src_ref=down_out.at[step], dst_ref=down_in.at[step], send_sem=down_send.at[step],
            recv_sem=down_recv.at[step], device_id={"col": jnp.maximum(col - 1, 0)},
            device_id_type=MESH,
        )

    def up(step):
        return pltpu.make_async_remote_copy(
            src_ref=up_out.at[step], dst_ref=up_in.at[step], send_sem=up_send.at[step],
            recv_sem=up_recv.at[step], device_id={"col": jnp.minimum(col + 1, cols - 1)},
            device_id_type=MESH,
        )

    to_partner(own_ref, 1).start()
    for d in range(1, chips):
        to_chip(d).start()

    owns = jnp.int32(0)
    for s in range(owner_ref.shape[0]):
        owns = owns + jnp.where(owner_ref[s] == col, 1, 0)
    tile_rows, tile_cols = tiles_ref.shape
    th, tw = kept.shape[0] // tile_rows, kept.shape[1] // tile_cols
    for i in range(tile_rows):
        for j in range(tile_cols):
            keep = (tiles_ref[i, j] * owns).astype(jnp.float32)
            part = amp_ref[i * th:(i + 1) * th, j * tw:(j + 1) * tw].astype(jnp.float32)
            kept[i * th:(i + 1) * th, j * tw:(j + 1) * tw] = (part * keep).astype(kept.dtype)
    held[0] = own_ref[...]
    out_ref[...] = jnp.zeros_like(out_ref)

    @pl.when(last)
    def _():
        down_in[...] = jnp.zeros_like(down_in)

    @pl.when(first)
    def _():
        up_in[...] = jnp.zeros_like(up_in)

    def body(i, carry):
        @pl.when(i < steps)
        def _():
            block, part = i // SPLITS, i % SPLITS

            @pl.when((part == 0) & (block > 0))
            def _():
                to_partner(own_ref, block).wait_recv()

                @pl.when(block % 2 == 0)
                def _():
                    to_partner(held.at[block], block + 1).start()

            local[i] = jnp.dot(
                kept[pl.ds(part * height, height), :], held[block],
                preferred_element_type=jnp.float32,
            )

        going_down = i - (cols - 1 - col) * SKEW

        @pl.when((going_down >= 0) & (going_down < steps))
        def _():
            @pl.when(col < cols - 1)
            def _():
                down(going_down).wait_recv()

            @pl.when(col > 0)
            def _():
                value = local[going_down] + down_in[going_down].astype(jnp.float32)
                down_out[going_down] = value.astype(down_out.dtype)
                down(going_down).start()

        going_up = i - col * SKEW

        @pl.when((going_up >= 0) & (going_up < steps))
        def _():
            @pl.when(col > 0)
            def _():
                up(going_up).wait_recv()

            @pl.when(col < cols - 1)
            def _():
                value = local[going_up] + up_in[going_up].astype(jnp.float32)
                up_out[going_up] = value.astype(up_out.dtype)
                up(going_up).start()

        done = i - (cols - 1) * SKEW

        @pl.when(done >= 0)
        def _():
            block, part = done // SPLITS, done % SPLITS
            value = local[done] + down_in[done].astype(jnp.float32) + up_in[done].astype(jnp.float32)
            rows = pl.ds(part * height, height)
            out_ref[rows, :] += lax.dot_general(
                value.astype(held.dtype), held[block], (((1,), (1,)), ((), ())),
                preferred_element_type=jnp.float32,
            )

        return carry

    lax.fori_loop(0, steps + (cols - 1) * SKEW, body, 0)

    for slot in range(1, blocks):
        to_partner(own_ref, slot).wait_send()

    def drain(i, carry):
        @pl.when(col > 0)
        def _():
            down(i).wait_send()

        @pl.when(col < cols - 1)
        def _():
            up(i).wait_send()

        return carry

    lax.fori_loop(0, steps, drain, 0)


def shards(row_count, col_count, amplitudes, factors, tile_map, panel_owner):
    rows, width = amplitudes.shape
    pairs, depth = factors.shape
    chips = row_count // 2
    blocks = row_count
    steps = blocks * SPLITS
    height = rows // SPLITS
    dma = pltpu.SemaphoreType.DMA
    chunk = (steps, height, depth)
    total = pl.pallas_call(
        functools.partial(kernel, col_count, chips),
        out_shape=jax.ShapeDtypeStruct((rows, pairs), jnp.float32),
        in_specs=[pl.BlockSpec(memory_space=pltpu.SMEM)] * 2 + [pl.BlockSpec(memory_space=pltpu.VMEM)] * 2,
        out_specs=pl.BlockSpec(memory_space=pltpu.VMEM),
        scratch_shapes=[
            pltpu.VMEM((blocks, pairs, depth), factors.dtype),
            pltpu.VMEM((rows, width), amplitudes.dtype),
            pltpu.VMEM(chunk, jnp.float32),
        ] + [pltpu.VMEM(chunk, jnp.bfloat16)] * 4 + [
            dma((blocks,)), dma((blocks,)),
            dma((steps,)), dma((steps,)), dma((steps,)), dma((steps,)),
        ],
        compiler_params=pltpu.CompilerParams(collective_id=0, has_side_effects=True),
    )(panel_owner, tile_map, amplitudes, factors)
    return keep_tiles(total, tile_map)


def solution(mesh):
    in_specs = (P("row", "col"), P("col", "row"), P("row", "col"), P())
    out_specs = P("row", "col")
    body = functools.partial(shards, mesh.shape["row"], mesh.shape["col"])
    return jax.shard_map(body, mesh=mesh, in_specs=in_specs, out_specs=out_specs, check_vma=False)
```

```python
import functools

import jax
import jax.numpy as jnp
from jax import lax
from jax.experimental import pallas as pl
from jax.experimental.pallas import tpu as pltpu
from jax.sharding import PartitionSpec as P

MESH = pl.DeviceIdType.MESH
SPLITS = 4
SKEW = 3
GRANT = 62 * 1024 * 1024


def flip(index, bits):
    bit = 1
    while bit <= bits:
        if bits & bit:
            index = index + bit - 2 * bit * ((index // bit) % 2)
        bit *= 2
    return index


def keep_tiles(block, tiles):
    rows, cols = tiles.shape
    keep = jnp.repeat(tiles.astype(block.dtype), block.shape[1] // cols, axis=1)
    shaped = block.reshape(rows, block.shape[0] // rows, block.shape[1])
    return (shaped * keep[:, None, :]).reshape(block.shape)


def kernel(
    cols, chips, owner_ref, tiles_ref, amp_ref, own_ref, out_ref,
    held, kept, local, down_out, down_in, up_out, up_in,
    held_send, held_recv, down_send, down_recv, up_send, up_recv,
):
    row, col = lax.axis_index("row"), lax.axis_index("col")
    core, chip = row % 2, row // 2
    partner = row + 1 - 2 * core
    blocks = 2 * chips
    steps = blocks * SPLITS
    height = kept.shape[0] // SPLITS
    first, last = col == 0, col == cols - 1

    barrier = pltpu.get_barrier_semaphore()

    def greet(**where):
        pl.semaphore_signal(barrier, inc=1, device_id=where, device_id_type=MESH)

    greet(row=partner)
    for d in range(1, chips):
        greet(row=2 * flip(chip, d) + core)

    @pl.when(col > 0)
    def _():
        greet(col=col - 1)

    @pl.when(col < cols - 1)
    def _():
        greet(col=col + 1)

    def to_partner(src, slot):
        return pltpu.make_async_remote_copy(
            src_ref=src, dst_ref=held.at[slot], send_sem=held_send.at[slot],
            recv_sem=held_recv.at[slot], device_id={"row": partner}, device_id_type=MESH,
        )

    def to_chip(d):
        return pltpu.make_async_remote_copy(
            src_ref=own_ref, dst_ref=held.at[2 * d], send_sem=held_send.at[2 * d],
            recv_sem=held_recv.at[2 * d], device_id={"row": 2 * flip(chip, d) + core},
            device_id_type=MESH,
        )

    def down(step):
        block, rows = chunk_of(step)
        return pltpu.make_async_remote_copy(
            src_ref=down_out.at[block, rows, :], dst_ref=down_in.at[block, rows, :], send_sem=down_send.at[step],
            recv_sem=down_recv.at[step], device_id={"col": jnp.maximum(col - 1, 0)},
            device_id_type=MESH,
        )

    def up(step):
        block, rows = chunk_of(step)
        return pltpu.make_async_remote_copy(
            src_ref=up_out.at[block, rows, :], dst_ref=up_in.at[block, rows, :], send_sem=up_send.at[step],
            recv_sem=up_recv.at[step], device_id={"col": jnp.minimum(col + 1, cols - 1)},
            device_id_type=MESH,
        )

    owns = jnp.int32(0)
    for s in range(owner_ref.shape[0]):
        owns = owns + jnp.where(owner_ref[s] == col, 1, 0)
    tile_rows, tile_cols = tiles_ref.shape
    th, tw = kept.shape[0] // tile_rows, kept.shape[1] // tile_cols
    for i in range(tile_rows):
        for j in range(tile_cols):
            keep = (tiles_ref[i, j] * owns).astype(jnp.float32)
            part = amp_ref[i * th:(i + 1) * th, j * tw:(j + 1) * tw].astype(jnp.float32)
            kept[i * th:(i + 1) * th, j * tw:(j + 1) * tw] = (part * keep).astype(kept.dtype)
    held[0] = own_ref[...]

    ends = jnp.where(first, 1, 0) + jnp.where(last, 1, 0)
    pl.semaphore_wait(barrier, chips + 2 - ends)
    to_partner(own_ref, 1).start()
    for d in range(1, chips):
        to_chip(d).start()

    def chunk_of(step):
        return step // SPLITS, pl.ds(pl.multiple_of(step % SPLITS * height, height), height)

    near = jnp.minimum(col, cols - 1 - col)

    def body(i, carry):
        made = i - near * SKEW

        @pl.when((made >= 0) & (made < steps) & (made % SPLITS == 0))
        def _():
            block = made // SPLITS

            @pl.when(block > 0)
            def _():
                to_partner(own_ref, block).wait_recv()

                @pl.when(block % 2 == 0)
                def _():
                    to_partner(held.at[block], block + 1).start()

            local[block] = jnp.dot(kept[...], held[block], preferred_element_type=jnp.float32)

        going_down = i - (cols - 1 - col) * SKEW

        @pl.when((going_down >= 0) & (going_down < steps))
        def _():
            block, rows = chunk_of(going_down)

            @pl.when(last)
            def _():
                down_in[block, rows, :] = jnp.zeros((height, down_in.shape[2]), down_in.dtype)

            @pl.when(col < cols - 1)
            def _():
                down(going_down).wait_recv()

            @pl.when(col > 0)
            def _():
                value = local[block, rows, :] + down_in[block, rows, :].astype(jnp.float32)
                down_out[block, rows, :] = value.astype(down_out.dtype)
                down(going_down).start()

        going_up = i - col * SKEW

        @pl.when((going_up >= 0) & (going_up < steps))
        def _():
            block, rows = chunk_of(going_up)

            @pl.when(first)
            def _():
                up_in[block, rows, :] = jnp.zeros((height, up_in.shape[2]), up_in.dtype)

            @pl.when(col > 0)
            def _():
                up(going_up).wait_recv()

            @pl.when(col < cols - 1)
            def _():
                value = local[block, rows, :] + up_in[block, rows, :].astype(jnp.float32)
                up_out[block, rows, :] = value.astype(up_out.dtype)
                up(going_up).start()

        done = i - (cols - 1) * SKEW

        @pl.when((done >= 0) & (done % SPLITS == SPLITS - 1))
        def _():
            block = done // SPLITS
            value = local[block] + down_in[block].astype(jnp.float32) + up_in[block].astype(jnp.float32)
            product = lax.dot_general(
                value.astype(held.dtype), held[block], (((1,), (1,)), ((), ())),
                preferred_element_type=jnp.float32,
            )

            @pl.when(block == 0)
            def _():
                out_ref[...] = product

            @pl.when(block > 0)
            def _():
                out_ref[...] += product

        return carry

    lax.fori_loop(0, steps + (cols - 1) * SKEW, body, 0)

    for slot in range(1, blocks):
        to_partner(own_ref, slot).wait_send()

    def drain(i, carry):
        @pl.when(col > 0)
        def _():
            down(i).wait_send()

        @pl.when(col < cols - 1)
        def _():
            up(i).wait_send()

        return carry

    lax.fori_loop(0, steps, drain, 0)


def shards(row_count, col_count, amplitudes, factors, tile_map, panel_owner):
    rows, width = amplitudes.shape
    pairs, depth = factors.shape
    chips = row_count // 2
    blocks = row_count
    steps = blocks * SPLITS
    dma = pltpu.SemaphoreType.DMA
    chunk = (blocks, rows, depth)
    total = pl.pallas_call(
        functools.partial(kernel, col_count, chips),
        out_shape=jax.ShapeDtypeStruct((rows, pairs), jnp.float32),
        in_specs=[pl.BlockSpec(memory_space=pltpu.SMEM)] * 2 + [pl.BlockSpec(memory_space=pltpu.VMEM)] * 2,
        out_specs=pl.BlockSpec(memory_space=pltpu.VMEM),
        scratch_shapes=[
            pltpu.VMEM((blocks, pairs, depth), factors.dtype),
            pltpu.VMEM((rows, width), amplitudes.dtype),
            pltpu.VMEM(chunk, jnp.float32),
        ] + [pltpu.VMEM(chunk, jnp.bfloat16)] * 4 + [
            dma((blocks,)), dma((blocks,)),
            dma((steps,)), dma((steps,)), dma((steps,)), dma((steps,)),
        ],
        compiler_params=pltpu.CompilerParams(collective_id=0, has_side_effects=True, vmem_limit_bytes=GRANT),
    )(panel_owner, tile_map, amplitudes, factors)
    return keep_tiles(total, tile_map)


def solution(mesh):
    in_specs = (P("row", "col"), P("col", "row"), P("row", "col"), P())
    out_specs = P("row", "col")
    body = functools.partial(shards, mesh.shape["row"], mesh.shape["col"])
    return jax.shard_map(body, mesh=mesh, in_specs=in_specs, out_specs=out_specs, check_vma=False)
```

```python
import functools

import jax
import jax.numpy as jnp
from jax import lax
from jax.experimental import pallas as pl
from jax.experimental.pallas import tpu as pltpu
from jax.sharding import PartitionSpec as P

MESH = pl.DeviceIdType.MESH
SPLITS = 4
SKEW = 3
GRANT = 62390272


def flip(index, bits):
    bit = 1
    while bit <= bits:
        if bits & bit:
            index = index + bit - 2 * bit * ((index // bit) % 2)
        bit *= 2
    return index


def keep_tiles(block, tiles):
    rows, cols = tiles.shape
    keep = jnp.repeat(tiles.astype(block.dtype), block.shape[1] // cols, axis=1)
    shaped = block.reshape(rows, block.shape[0] // rows, block.shape[1])
    return (shaped * keep[:, None, :]).reshape(block.shape)


def kernel(
    cols, chips, owner_ref, tiles_ref, amp_ref, own_ref, out_ref,
    held, kept, local, down_out, down_in, up_out, up_in,
    held_send, held_recv, down_send, down_recv, up_send, up_recv,
):
    row, col = lax.axis_index("row"), lax.axis_index("col")
    core, chip = row % 2, row // 2
    partner = row + 1 - 2 * core
    blocks = 2 * chips
    steps = blocks * SPLITS
    height = kept.shape[0] // SPLITS
    first, last = col == 0, col == cols - 1

    barrier = pltpu.get_barrier_semaphore()

    def greet(**where):
        pl.semaphore_signal(barrier, inc=1, device_id=where, device_id_type=MESH)

    greet(row=partner)
    for d in range(1, chips):
        greet(row=2 * flip(chip, d) + core)

    @pl.when(col > 0)
    def _():
        greet(col=col - 1)

    @pl.when(col < cols - 1)
    def _():
        greet(col=col + 1)

    def to_partner(src, slot):
        return pltpu.make_async_remote_copy(
            src_ref=src, dst_ref=held.at[slot], send_sem=held_send.at[slot],
            recv_sem=held_recv.at[slot], device_id={"row": partner}, device_id_type=MESH,
        )

    def to_chip(d):
        return pltpu.make_async_remote_copy(
            src_ref=own_ref, dst_ref=held.at[2 * d], send_sem=held_send.at[2 * d],
            recv_sem=held_recv.at[2 * d], device_id={"row": 2 * flip(chip, d) + core},
            device_id_type=MESH,
        )

    def down(step):
        block, rows = chunk_of(step)
        return pltpu.make_async_remote_copy(
            src_ref=down_out.at[block, rows, :], dst_ref=down_in.at[block, rows, :], send_sem=down_send.at[step],
            recv_sem=down_recv.at[step], device_id={"col": jnp.maximum(col - 1, 0)},
            device_id_type=MESH,
        )

    def up(step):
        block, rows = chunk_of(step)
        return pltpu.make_async_remote_copy(
            src_ref=up_out.at[block, rows, :], dst_ref=up_in.at[block, rows, :], send_sem=up_send.at[step],
            recv_sem=up_recv.at[step], device_id={"col": jnp.minimum(col + 1, cols - 1)},
            device_id_type=MESH,
        )

    owns = jnp.int32(0)
    for s in range(owner_ref.shape[0]):
        owns = owns + jnp.where(owner_ref[s] == col, 1, 0)
    tile_rows, tile_cols = tiles_ref.shape
    th, tw = kept.shape[0] // tile_rows, kept.shape[1] // tile_cols
    for i in range(tile_rows):
        for j in range(tile_cols):
            keep = (tiles_ref[i, j] * owns).astype(jnp.float32)
            part = amp_ref[i * th:(i + 1) * th, j * tw:(j + 1) * tw].astype(jnp.float32)
            kept[i * th:(i + 1) * th, j * tw:(j + 1) * tw] = (part * keep).astype(kept.dtype)
    held[0] = own_ref[...]

    ends = jnp.where(first, 1, 0) + jnp.where(last, 1, 0)
    pl.semaphore_wait(barrier, chips + 2 - ends)
    to_partner(own_ref, 1).start()
    for d in range(1, chips):
        to_chip(d).start()

    def chunk_of(step):
        return step // SPLITS, pl.ds(pl.multiple_of(step % SPLITS * height, height), height)

    near = jnp.minimum(col, cols - 1 - col)

    def body(i, carry):
        made = i - near * SKEW

        @pl.when((made >= 0) & (made < steps) & (made % SPLITS == 0))
        def _():
            block = made // SPLITS

            @pl.when(block > 0)
            def _():
                to_partner(own_ref, block).wait_recv()

                @pl.when(block % 2 == 0)
                def _():
                    to_partner(held.at[block], block + 1).start()

            local[block] = jnp.dot(kept[...], held[block], preferred_element_type=jnp.float32)

        going_down = i - (cols - 1 - col) * SKEW

        @pl.when((going_down >= 0) & (going_down < steps))
        def _():
            block, rows = chunk_of(going_down)

            @pl.when(last)
            def _():
                down_in[block, rows, :] = jnp.zeros((height, down_in.shape[2]), down_in.dtype)

            @pl.when(col < cols - 1)
            def _():
                down(going_down).wait_recv()

            @pl.when(col > 0)
            def _():
                value = local[block, rows, :] + down_in[block, rows, :].astype(jnp.float32)
                down_out[block, rows, :] = value.astype(down_out.dtype)
                down(going_down).start()

        going_up = i - col * SKEW

        @pl.when((going_up >= 0) & (going_up < steps))
        def _():
            block, rows = chunk_of(going_up)

            @pl.when(first)
            def _():
                up_in[block, rows, :] = jnp.zeros((height, up_in.shape[2]), up_in.dtype)

            @pl.when(col > 0)
            def _():
                up(going_up).wait_recv()

            @pl.when(col < cols - 1)
            def _():
                value = local[block, rows, :] + up_in[block, rows, :].astype(jnp.float32)
                up_out[block, rows, :] = value.astype(up_out.dtype)
                up(going_up).start()

        done = i - (cols - 1) * SKEW

        @pl.when((done >= 0) & (done % SPLITS == SPLITS - 1))
        def _():
            block = done // SPLITS
            value = local[block] + down_in[block].astype(jnp.float32) + up_in[block].astype(jnp.float32)
            product = lax.dot_general(
                value.astype(held.dtype), held[block], (((1,), (1,)), ((), ())),
                preferred_element_type=jnp.float32,
            )

            @pl.when(block == 0)
            def _():
                out_ref[...] = product

            @pl.when(block > 0)
            def _():
                out_ref[...] += product

        return carry

    lax.fori_loop(0, steps + (cols - 1) * SKEW, body, 0)

    for slot in range(1, blocks):
        to_partner(own_ref, slot).wait_send()

    def drain(i, carry):
        @pl.when(col > 0)
        def _():
            down(i).wait_send()

        @pl.when(col < cols - 1)
        def _():
            up(i).wait_send()

        return carry

    lax.fori_loop(0, steps, drain, 0)


def shards(row_count, col_count, amplitudes, factors, tile_map, panel_owner):
    rows, width = amplitudes.shape
    pairs, depth = factors.shape
    chips = row_count // 2
    blocks = row_count
    steps = blocks * SPLITS
    dma = pltpu.SemaphoreType.DMA
    chunk = (blocks, rows, depth)
    total = pl.pallas_call(
        functools.partial(kernel, col_count, chips),
        out_shape=pltpu.VMEM((rows, pairs), jnp.float32),
        in_specs=[pl.BlockSpec(memory_space=pltpu.SMEM)] * 2 + [pl.BlockSpec(memory_space=pltpu.VMEM)] * 2,
        out_specs=pl.BlockSpec(memory_space=pltpu.VMEM),
        scratch_shapes=[
            pltpu.VMEM((blocks, pairs, depth), factors.dtype),
            pltpu.VMEM((rows, width), amplitudes.dtype),
            pltpu.VMEM(chunk, jnp.float32),
        ] + [pltpu.VMEM(chunk, jnp.bfloat16)] * 4 + [
            dma((blocks,)), dma((blocks,)),
            dma((steps,)), dma((steps,)), dma((steps,)), dma((steps,)),
        ],
        compiler_params=pltpu.CompilerParams(collective_id=0, has_side_effects=True, vmem_limit_bytes=GRANT),
    )(panel_owner, tile_map, amplitudes, factors)
    return keep_tiles(total, tile_map)


def solution(mesh):
    in_specs = (P("row", "col"), P("col", "row"), P("row", "col"), P())
    out_specs = P("row", "col")
    body = functools.partial(shards, mesh.shape["row"], mesh.shape["col"])
    return jax.shard_map(body, mesh=mesh, in_specs=in_specs, out_specs=out_specs, check_vma=False)
```
